256 devices in a mesh: bin: 64 (over x, z_hi, y, core), dp: 4 (over z_lo).
Axes of the slice: x: 4, y: 4, z: 8 (z_hi: 2, z_lo: 4; z = z_hi * 4 + z_lo), core: 2. Of those that a mesh axis runs over, the one named last changes fastest.
Arguments:
- peak_bins: int32 [512, 128], P('dp'), may hold values from 0 to 196607
- peak_values: bfloat16 [512, 128], P('dp'), may hold values from 0.049804688 to 1
- enc_weight: bfloat16 [196608, 2048], P(('bin', 'dp')), may hold values from -0.5 to 0.5
- enc_bias: float32 [2048], replicated, may hold values from -3 to 3
- dec_weight: bfloat16 [2048, 196608], P(None, ('bin', 'dp')), may hold values from -0.0007324219 to 0.0007324219
Outputs:
- grad_enc: bfloat16 [196608, 2048], P(('bin', 'dp'))
- grad_dec: bfloat16 [2048, 196608], P(None, ('bin', 'dp'))
The draws below stay inside these ranges and needn't reach their ends.
All inputs are finite; a program needn't handle non-finite values.
Results may differ from the reference program's by a relative error of at most 0.0057.
Values may be sent and summed in bfloat16 or wider, within the bound.
No kernel may reach another device: no remote copies, remote signals or barrier semaphores. Data moves between devices by JAX's collectives and lax.ppermute only.
A program may use at most 64 MiB of HBM per device.

```python
import math
import jax
import jax.numpy as jnp

BINS = 196608
HIDDEN_SIZE = 2048
PEAKS = 128
SPECTRA = 512


def plant(values, rng, smallest, top_value):
    place = [jax.random.randint(jax.random.fold_in(rng, axis), (), 0, length) for axis, length in enumerate(values.shape)]
    widest = values.shape.index(max(values.shape))
    neighbour = place[:widest] + [(place[widest] + 1) % values.shape[widest]] + place[widest + 1:]
    return values.at[tuple(place)].set(smallest).at[tuple(neighbour)].set(top_value)


def steps_of(key, shape, shards, low, largest):
    gain, own = 1.0, jax.random.fold_in(key, 6)
    for position, shards_of in shards:
        heights = jnp.exp(jax.random.uniform(jax.random.fold_in(own, position), (shards_of,), jnp.float32, low / len(shards), largest / len(shards)))
        gain = gain * jnp.repeat(heights, shape[position] // shards_of).reshape([-1 if axis == position else 1 for axis in range(len(shape))])
    return gain


def bell_draw(key, shape, deviation, limit, cuts=(), kind=jnp.bfloat16):
    array = jax.random.normal(key, shape, jnp.float32) * deviation
    if len(cuts) > 0:
        array = steps_of(key, shape, cuts, -0.22, 0.18) * array
    return jnp.clip(array, min=-limit, max=limit).astype(kind)


def setup_inputs(seed: int = 0) -> dict:
    streams_of = jax.random.split(jax.random.key(seed), 6)
    peak_bins = plant(jax.random.randint(streams_of[0], (SPECTRA, PEAKS), 0, BINS), jax.random.fold_in(streams_of[0], 1), 0, BINS - 1).astype(jnp.int32)
    peak_values = jnp.clip(jnp.exp(math.log(1.0) - 2.9996462 * jax.random.uniform(streams_of[1], (SPECTRA, PEAKS), jnp.float32) ** steps_of(streams_of[1], (SPECTRA, PEAKS), ((0, 4),), -0.2, 0.2)), 0.049804688, 1.0).astype(jnp.bfloat16)
    enc_weight = bell_draw(streams_of[2], (BINS, HIDDEN_SIZE), PEAKS ** -0.5, 0.5, ((0, 256),))
    enc_bias = bell_draw(streams_of[3], (HIDDEN_SIZE,), 0.5, 3.0, (), jnp.float32)
    dec_weight = bell_draw(streams_of[4], (HIDDEN_SIZE, BINS), (2.0 * PEAKS ** 0.5 / BINS), 0.0007324219, ((1, 256),))
    return {"peak_bins": peak_bins, "peak_values": peak_values, "enc_weight": enc_weight, "enc_bias": enc_bias, "dec_weight": dec_weight}


def activation(values):
    return jax.nn.gelu(values, approximate=True)

def reference(peak_bins, peak_values, enc_weight, enc_bias, dec_weight):
    row_ids = jnp.broadcast_to(jnp.arange(SPECTRA, dtype=jnp.int32)[:, None], peak_bins.shape)
    dense = jnp.zeros((SPECTRA, BINS), jnp.float32).at[row_ids, peak_bins].add(peak_values.astype(jnp.float32)).astype(jnp.bfloat16)
    pre = jnp.dot(dense, enc_weight, preferred_element_type=jnp.float32) + enc_bias
    hidden = activation(pre).astype(jnp.bfloat16)
    recon = jnp.dot(hidden, dec_weight, preferred_element_type=jnp.float32)
    resid = (recon - dense.astype(jnp.float32)).astype(jnp.bfloat16)
    grad_dec = jnp.dot(hidden.T, resid, preferred_element_type=jnp.float32).astype(jnp.bfloat16)
    back = jnp.dot(resid, dec_weight.T, preferred_element_type=jnp.float32)
    _, pullback = jax.vjp(activation, pre)
    dpre = pullback(back)[0].astype(jnp.bfloat16)
    grad_enc = jnp.dot(dense.T, dpre, preferred_element_type=jnp.float32).astype(jnp.bfloat16)
    return (grad_enc, grad_dec)
```

```python
import functools

import jax
import jax.numpy as jnp
from jax import lax
from jax.experimental import pallas as pl
from jax.experimental.pallas import tpu as pltpu
from jax.sharding import Mesh
from jax.sharding import PartitionSpec as P

SHAPE = (4, 2, 4, 2, 4)
NAMES = ("x", "zhi", "y", "core", "zlo")
PLANE = ("x", "y")
DEPTH = ("zhi", "zlo")
LANES = 128
BF16 = jnp.bfloat16
F32 = jnp.float32


def activation(values):
    return jax.nn.gelu(values, approximate=True)


def slope_times(pre, back):
    _, pullback = jax.vjp(activation, pre)
    return pullback(back)[0].astype(BF16)


def dense_kernel(place_ref, peaks_ref, out_ref, *, peaks):
    rows, width = out_ref.shape
    tiles = width // LANES
    first, shift = place_ref[0], place_ref[1]
    lane = lax.broadcasted_iota(jnp.int32, (LANES, 1), 0).astype(BF16)
    sub = lax.broadcasted_iota(jnp.int32, (8, 1), 0)

    def step(group, carry):
        row = pl.multiple_of(group * 16, 16)
        source = pl.multiple_of(lax.rem(row + shift, rows), 16)
        local = peaks_ref[pl.ds(source, 16), :peaks].astype(jnp.int32) - first
        values = peaks_ref[pl.ds(source, 16), peaks:]
        high = local >> 7
        low = (local & (LANES - 1)).astype(BF16)
        halves = []
        for half in (0, 8):
            picked = [
                jnp.where(high[half : half + 8] == tile, values[half : half + 8], 0.0)
                for tile in range(tiles)
            ]
            total = None
            for pair in range(0, 8, 2):
                left = jnp.concatenate(
                    [
                        jnp.concatenate([jnp.where(sub == s, one, 0.0) for one in picked], axis=0)
                        for s in (pair, pair + 1)
                    ],
                    axis=1,
                ).astype(BF16)
                right = jnp.concatenate(
                    [
                        jnp.where(low[half + s][None, :] == lane, 1.0, 0.0).astype(BF16)
                        for s in (pair, pair + 1)
                    ],
                    axis=1,
                )
                term = lax.dot_general(
                    left, right, (((1,), (1,)), ((), ())), preferred_element_type=F32
                )
                total = term if total is None else total + term
            halves.append(total)
        for tile in range(tiles):
            block = jnp.concatenate(
                [total[tile * 8 : tile * 8 + 8] for total in halves], axis=0
            )
            out_ref[pl.ds(row, 16), tile * LANES : (tile + 1) * LANES] = block.astype(BF16)
        return carry

    lax.fori_loop(0, rows // 16, step, 0, unroll=4)


def build_dense(place, packed, width):
    rows, lanes = packed.shape
    return pl.pallas_call(
        functools.partial(dense_kernel, peaks=lanes // 2),
        out_shape=jax.ShapeDtypeStruct((rows, width), BF16),
        in_specs=[
            pl.BlockSpec(memory_space=pltpu.SMEM),
            pl.BlockSpec(memory_space=pltpu.VMEM),
        ],
        out_specs=pl.BlockSpec(memory_space=pltpu.VMEM),
        compiler_params=pltpu.CompilerParams(vmem_limit_bytes=32 << 20),
        name="build_dense",
    )(place, packed)


def swap(values):
    return lax.ppermute(values, "core", [(0, 1), (1, 0)])


def exchange(values, axes):
    return lax.all_to_all(values, axes, 0, 0, tiled=True)


def gather(values, axes):
    count = lax.axis_size(axes)
    sent = jnp.broadcast_to(values[None], (count,) + values.shape)
    return exchange(sent, axes).reshape(-1, values.shape[-1])


def scatter_sum(own, other):
    hidden = own.shape[1]
    half = own + swap(other.astype(BF16)).astype(F32)
    plane = exchange(half.astype(BF16).reshape(16, -1, hidden), PLANE).astype(F32).sum(0)
    depth = exchange(plane.reshape(8, -1, hidden), DEPTH)
    return depth.sum(0)


def gather_rows(values):
    own = gather(gather(values, DEPTH), PLANE)
    return own, swap(own)


def on_device(peak_bins, peak_values, enc_weight, enc_bias, dec_weight):
    width = enc_weight.shape[0]
    position = lax.axis_index("x")
    for name in NAMES[1:]:
        position = position * lax.axis_size(name) + lax.axis_index(name)
    packed = gather(
        jnp.concatenate([peak_bins.astype(F32), peak_values.astype(F32)], axis=1), "zlo"
    )
    rows = packed.shape[0]
    part = rows // 2
    place = jnp.stack([position * width, lax.axis_index("core") * part]).astype(jnp.int32)
    dense = build_dense(place, packed, width)
    dense_own, dense_other = dense[:part], dense[part:]

    def encode(block):
        return jnp.dot(block, enc_weight, preferred_element_type=F32)

    def residual(block, hidden):
        recon = jnp.dot(hidden, dec_weight, preferred_element_type=F32)
        return (recon - block.astype(F32)).astype(BF16)

    def decode_back(resid):
        return lax.dot_general(
            resid, dec_weight, (((1,), (1,)), ((), ())), preferred_element_type=F32
        )

    def weight_grad(left, right):
        return lax.dot_general(
            left, right, (((0,), (0,)), ((), ())), preferred_element_type=F32
        ).astype(BF16)

    pre = scatter_sum(encode(dense_own), encode(dense_other)) + enc_bias
    hidden_own, hidden_other = gather_rows(activation(pre).astype(BF16))
    resid_own = residual(dense_own, hidden_own)
    resid_other = residual(dense_other, hidden_other)
    back = scatter_sum(decode_back(resid_own), decode_back(resid_other))
    grad_dec = weight_grad(
        jnp.concatenate([hidden_own, hidden_other]), jnp.concatenate([resid_own, resid_other])
    )
    dpre = jnp.concatenate(gather_rows(slope_times(pre, back)))
    grad_enc = weight_grad(dense, dpre)
    return (grad_enc, grad_dec)


def solution(mesh):
    fine = Mesh(mesh.devices.reshape(SHAPE), NAMES)
    bins = ("x", "zhi", "y", "core", "zlo")
    placed = (P("zlo", None), P("zlo", None), P(bins, None), P(), P(None, bins))
    return jax.shard_map(
        on_device,
        mesh=fine,
        in_specs=placed,
        out_specs=(P(bins, None), P(None, bins)),
        check_vma=False,
    )
```

```python
import functools

import jax
import jax.numpy as jnp
from jax import lax
from jax.experimental import pallas as pl
from jax.experimental.pallas import tpu as pltpu
from jax.sharding import Mesh
from jax.sharding import PartitionSpec as P

SHAPE = (4, 2, 4, 2, 2, 2)
NAMES = ("x", "zhi", "y", "core", "zp", "zq")
NEAR = ("x", "y", "zq")
FAR = ("zhi", "zp")
SPECTRA_AXES = ("zp", "zq")
LANES = 128
STEP = 512
BF16 = jnp.bfloat16
F32 = jnp.float32


def activation(values):
    return jax.nn.gelu(values, approximate=True)


def slope_times(pre, back):
    _, pullback = jax.vjp(activation, pre)
    return pullback(back)[0].astype(BF16)


def pack_kernel(core_ref, bins_ref, values_ref, out_ref):
    rows, lanes = out_ref.shape
    peaks = lanes // 3
    first = pl.multiple_of(core_ref[0] * rows, rows)
    bins = bins_ref[pl.ds(first, rows), :]
    out_ref[:, :peaks] = ((bins >> 9) - 192).astype(F32).astype(BF16)
    out_ref[:, peaks : 2 * peaks] = ((bins & (STEP - 1)) - 256).astype(F32).astype(BF16)
    out_ref[:, 2 * peaks :] = values_ref[pl.ds(first, rows), :]


def pack_peaks(core, bins, values):
    rows, peaks = bins.shape
    vmem = pl.BlockSpec(memory_space=pltpu.VMEM)
    return pl.pallas_call(
        pack_kernel,
        out_shape=jax.ShapeDtypeStruct((rows // 2, 3 * peaks), BF16),
        in_specs=[pl.BlockSpec(memory_space=pltpu.SMEM), vmem, vmem],
        out_specs=vmem,
        compiler_params=pltpu.CompilerParams(vmem_limit_bytes=4 << 20),
        name="pack_peaks",
    )(core, bins, values)


def dense_rows(bins, values, firsts, tiles, consts):
    lane, upper, which = consts
    low = (bins & (LANES - 1)).astype(BF16)
    twice = jnp.concatenate([values, values], axis=0).astype(BF16)
    picked = []
    for first in firsts:
        local = bins - first
        inside = (local >= 0) & (local < tiles * LANES)
        high = jnp.where(inside, local >> 7, -9).astype(F32)
        high = jnp.concatenate([high, high], axis=0).astype(BF16) - upper
        for tile in range(0, tiles, 2):
            picked.append(jnp.where(high == tile, twice, jnp.zeros_like(twice)))
    left = jnp.concatenate(
        [
            jnp.concatenate(
                [jnp.where(which == row, one, jnp.zeros_like(one)) for one in picked], axis=0
            )
            for row in range(8)
        ],
        axis=1,
    )
    ones = jnp.ones((LANES, LANES), BF16)
    right = jnp.concatenate(
        [jnp.where(low[row][None, :] == lane, ones, jnp.zeros_like(ones)) for row in range(8)],
        axis=1,
    )
    return lax.dot_general(left, right, (((1,), (1,)), ((), ())), preferred_element_type=F32)


def dense_kernel(place_ref, *refs, groups):
    packed_refs, (own_ref, other_ref) = refs[:groups], refs[groups:]
    peaks = packed_refs[0].shape[1] // 3
    rows = packed_refs[0].shape[0]
    tiles = own_ref.shape[1] // LANES
    firsts = (place_ref[0], place_ref[1])
    lane = lax.broadcasted_iota(jnp.int32, (LANES, 1), 0).astype(BF16)
    row16 = lax.broadcasted_iota(jnp.int32, (16, LANES), 0)
    consts = (lane, (row16 >= 8).astype(jnp.int32).astype(BF16), (row16 & 7).astype(BF16))
    for back, packed_ref in enumerate(packed_refs):
        base = lax.rem(place_ref[2] + groups - back, groups) * rows

        def step(group, carry, packed_ref=packed_ref, base=base):
            row = pl.multiple_of(group * 16, 16)
            block = packed_ref[pl.ds(row, 16), :].astype(F32)
            bins = (block[:, :peaks].astype(jnp.int32) + 192) * STEP
            bins = bins + block[:, peaks : 2 * peaks].astype(jnp.int32) + 256
            values = block[:, 2 * peaks :]
            sums = [
                dense_rows(bins[h : h + 8], values[h : h + 8], firsts, tiles, consts)
                for h in (0, 8)
            ]
            target = pl.multiple_of(base + row, 16)
            for ref, skip in ((own_ref, 0), (other_ref, tiles)):
                for tile in range(tiles):
                    at = (skip + tile) * 8
                    ref[pl.ds(target, 16), tile * LANES : (tile + 1) * LANES] = jnp.concatenate(
                        [one[at : at + 8] for one in sums], axis=0
                    ).astype(BF16)
            return carry

        lax.fori_loop(0, rows // 16, step, 0, unroll=True)


def build_dense(place, blocks, width):
    rows = blocks[0].shape[0] * len(blocks)
    vmem = pl.BlockSpec(memory_space=pltpu.VMEM)
    return pl.pallas_call(
        functools.partial(dense_kernel, groups=len(blocks)),
        out_shape=(jax.ShapeDtypeStruct((rows, width), BF16),) * 2,
        in_specs=[pl.BlockSpec(memory_space=pltpu.SMEM)] + [vmem] * len(blocks),
        out_specs=(vmem, vmem),
        compiler_params=pltpu.CompilerParams(vmem_limit_bytes=8 << 20),
        name="build_dense",
    )(place, *blocks)


def sum_kernel(parts_ref, out_ref):
    count, _, columns = parts_ref.shape
    block = 4 * LANES
    for first in range(0, columns, block):
        at = slice(first, first + block)
        total = parts_ref[0, :, at].astype(F32)
        for part in range(1, count):
            total = total + parts_ref[part, :, at].astype(F32)
        out_ref[:, at] = total.astype(out_ref.dtype)


def sum_parts(parts):
    vmem = pl.BlockSpec(memory_space=pltpu.VMEM)
    return pl.pallas_call(
        sum_kernel,
        out_shape=jax.ShapeDtypeStruct(parts.shape[1:], BF16),
        in_specs=[vmem],
        out_specs=vmem,
        compiler_params=pltpu.CompilerParams(vmem_limit_bytes=4 << 20),
        name="sum_parts",
    )(parts)


def swap(values):
    return lax.ppermute(values, "core", [(0, 1), (1, 0)])


def from_others(values, axes):
    count = lax.axis_size(axes)
    return [
        lax.ppermute(values, axes, [(i, (i + step) % count) for i in range(count)])
        for step in range(1, count)
    ]


def near_exchange(values):
    return lax.all_to_all(values, NEAR, 0, 0, tiled=True)


def far_sum(sent):
    one, two, three = [block.astype(F32) for block in from_others(sent, FAR)]
    return (sent.astype(F32) + two) + (one + three)


def near_gather(values):
    count = lax.axis_size(NEAR)
    sent = jnp.broadcast_to(values[None], (count,) + values.shape)
    return near_exchange(sent).reshape(-1, values.shape[-1])


def on_device(peak_bins, peak_values, enc_weight, enc_bias, dec_weight):
    width, hidden_size = enc_weight.shape
    core = lax.axis_index("core")
    group = lax.axis_index(SPECTRA_AXES)
    position = lax.axis_index(NAMES)
    stride = lax.axis_size(SPECTRA_AXES)
    partner = position + (1 - 2 * core) * stride
    place = jnp.stack([position * width, partner * width, group]).astype(jnp.int32)
    packed = pack_peaks(core.reshape(1), peak_bins, peak_values)
    dense_own, dense_sent = build_dense(
        place, [packed] + from_others(packed, SPECTRA_AXES), width
    )
    dense_other = swap(dense_sent)

    def encode(block):
        return jnp.dot(block, enc_weight, preferred_element_type=F32)

    def residual(block, hidden):
        recon = jnp.dot(hidden, dec_weight, preferred_element_type=F32)
        return (recon - block.astype(F32)).astype(BF16)

    def decode_back(resid):
        return lax.dot_general(
            resid, dec_weight, (((1,), (1,)), ((), ())), preferred_element_type=F32
        )

    def rows_dot(left, right):
        return lax.dot_general(
            left, right, (((0,), (0,)), ((), ())), preferred_element_type=F32
        )

    def near_parts(own, other):
        half = own + swap(other.astype(BF16)).astype(F32)
        return near_exchange(half.astype(BF16).reshape(lax.axis_size(NEAR), -1, hidden_size))

    parts = near_parts(encode(dense_own), encode(dense_other))
    pre = far_sum(sum_parts(parts)) + enc_bias
    hidden_own = near_gather(activation(pre).astype(BF16))
    hidden_other = swap(hidden_own)
    resid_own = residual(dense_own, hidden_own)
    resid_other = residual(dense_other, hidden_other)
    parts = near_parts(decode_back(resid_own), decode_back(resid_other))
    grad_dec = rows_dot(
        jnp.concatenate([hidden_own, hidden_other]), jnp.concatenate([resid_own, resid_other])
    ).astype(BF16)
    parts, grad_dec = lax.optimization_barrier((parts, grad_dec))
    back = far_sum(sum_parts(parts))
    dpre_own = near_gather(slope_times(pre, back))
    dpre_other = swap(dpre_own)
    grad_enc = (rows_dot(dense_own, dpre_own) + rows_dot(dense_other, dpre_other)).astype(BF16)
    return (grad_enc, grad_dec)


def solution(mesh):
    fine = Mesh(mesh.devices.reshape(SHAPE), NAMES)
    placed = (
        P(SPECTRA_AXES, None),
        P(SPECTRA_AXES, None),
        P(NAMES, None),
        P(),
        P(None, NAMES),
    )
    return jax.shard_map(
        on_device,
        mesh=fine,
        in_specs=placed,
        out_specs=(P(NAMES, None), P(None, NAMES)),
        check_vma=False,
    )
```

```python
import functools

import jax
import jax.numpy as jnp
from jax import lax
from jax.experimental import pallas as pl
from jax.experimental.pallas import tpu as pltpu
from jax.sharding import Mesh
from jax.sharding import PartitionSpec as P

SHAPE = (4, 2, 4, 2, 2, 2)
NAMES = ("x", "zhi", "y", "core", "zp", "zq")
NEAR = ("x", "y", "zq")
FAR = ("zhi", "zp")
SPECTRA_AXES = ("zp", "zq")
LANES = 128
STEP = 512
BF16 = jnp.bfloat16
F32 = jnp.float32


def activation(values):
    return jax.nn.gelu(values, approximate=True)


def slope_times(pre, back):
    _, pullback = jax.vjp(activation, pre)
    return pullback(back)[0].astype(BF16)


def pack_kernel(core_ref, bins_ref, values_ref, out_ref):
    rows, lanes = out_ref.shape
    peaks = lanes // 3
    first = pl.multiple_of(core_ref[0] * rows, rows)
    bins = bins_ref[pl.ds(first, rows), :]
    out_ref[:, :peaks] = ((bins >> 9) - 192).astype(F32).astype(BF16)
    out_ref[:, peaks : 2 * peaks] = ((bins & (STEP - 1)) - 256).astype(F32).astype(BF16)
    out_ref[:, 2 * peaks :] = values_ref[pl.ds(first, rows), :]


def pack_peaks(core, bins, values):
    rows, peaks = bins.shape
    vmem = pl.BlockSpec(memory_space=pltpu.VMEM)
    return pl.pallas_call(
        pack_kernel,
        out_shape=jax.ShapeDtypeStruct((rows // 2, 3 * peaks), BF16),
        in_specs=[pl.BlockSpec(memory_space=pltpu.SMEM), vmem, vmem],
        out_specs=vmem,
        compiler_params=pltpu.CompilerParams(vmem_limit_bytes=4 << 20),
        name="pack_peaks",
    )(core, bins, values)


def dense_rows(bins, values, firsts, tiles, consts):
    lane, upper, which = consts
    low = (bins & (LANES - 1)).astype(BF16)
    twice = jnp.concatenate([values, values], axis=0).astype(BF16)
    picked = []
    for first in firsts:
        local = bins - first
        inside = (local >= 0) & (local < tiles * LANES)
        high = jnp.where(inside, local >> 7, -9).astype(F32)
        high = jnp.concatenate([high, high], axis=0).astype(BF16) - upper
        for tile in range(0, tiles, 2):
            picked.append(jnp.where(high == tile, twice, jnp.zeros_like(twice)))
    left = jnp.concatenate(
        [
            jnp.concatenate(
                [jnp.where(which == row, one, jnp.zeros_like(one)) for one in picked], axis=0
            )
            for row in range(8)
        ],
        axis=1,
    )
    ones = jnp.ones((LANES, LANES), BF16)
    right = jnp.concatenate(
        [jnp.where(low[row][None, :] == lane, ones, jnp.zeros_like(ones)) for row in range(8)],
        axis=1,
    )
    return lax.dot_general(left, right, (((1,), (1,)), ((), ())), preferred_element_type=F32)


def dense_kernel(place_ref, *refs, groups):
    packed_refs, (own_ref, other_ref) = refs[:groups], refs[groups:]
    peaks = packed_refs[0].shape[1] // 3
    rows = packed_refs[0].shape[0]
    tiles = own_ref.shape[1] // LANES
    firsts = (place_ref[0], place_ref[1])
    lane = lax.broadcasted_iota(jnp.int32, (LANES, 1), 0).astype(BF16)
    row16 = lax.broadcasted_iota(jnp.int32, (16, LANES), 0)
    consts = (lane, (row16 >= 8).astype(jnp.int32).astype(BF16), (row16 & 7).astype(BF16))
    for back, packed_ref in enumerate(packed_refs):
        base = lax.rem(place_ref[2] + groups - back, groups) * rows

        def step(group, carry, packed_ref=packed_ref, base=base):
            row = pl.multiple_of(group * 16, 16)
            block = packed_ref[pl.ds(row, 16), :].astype(F32)
            bins = (block[:, :peaks].astype(jnp.int32) + 192) * STEP
            bins = bins + block[:, peaks : 2 * peaks].astype(jnp.int32) + 256
            values = block[:, 2 * peaks :]
            sums = [
                dense_rows(bins[h : h + 8], values[h : h + 8], firsts, tiles, consts)
                for h in (0, 8)
            ]
            target = pl.multiple_of(base + row, 16)
            for ref, skip in ((own_ref, 0), (other_ref, tiles)):
                for tile in range(tiles):
                    at = (skip + tile) * 8
                    ref[pl.ds(target, 16), tile * LANES : (tile + 1) * LANES] = jnp.concatenate(
                        [one[at : at + 8] for one in sums], axis=0
                    ).astype(BF16)
            return carry

        lax.fori_loop(0, rows // 16, step, 0, unroll=True)


def build_dense(place, blocks, width):
    rows = blocks[0].shape[0] * len(blocks)
    vmem = pl.BlockSpec(memory_space=pltpu.VMEM)
    return pl.pallas_call(
        functools.partial(dense_kernel, groups=len(blocks)),
        out_shape=(jax.ShapeDtypeStruct((rows, width), BF16),) * 2,
        grid=(1,),
        in_specs=[pl.BlockSpec(memory_space=pltpu.SMEM)]
        + [pl.BlockSpec(block.shape, lambda i: (0, 0)) for block in blocks],
        out_specs=(vmem, vmem),
        compiler_params=pltpu.CompilerParams(vmem_limit_bytes=8 << 20),
        name="build_dense",
    )(place, *blocks)


def sum_kernel(parts_ref, out_ref):
    count, _, columns = parts_ref.shape
    block = 4 * LANES
    for first in range(0, columns, block):
        at = slice(first, first + block)
        total = parts_ref[0, :, at].astype(F32)
        for part in range(1, count):
            total = total + parts_ref[part, :, at].astype(F32)
        out_ref[:, at] = total.astype(out_ref.dtype)


def sum_parts(parts):
    vmem = pl.BlockSpec(memory_space=pltpu.VMEM)
    return pl.pallas_call(
        sum_kernel,
        out_shape=jax.ShapeDtypeStruct(parts.shape[1:], BF16),
        in_specs=[vmem],
        out_specs=vmem,
        compiler_params=pltpu.CompilerParams(vmem_limit_bytes=4 << 20),
        name="sum_parts",
    )(parts)


def swap(values):
    return lax.ppermute(values, "core", [(0, 1), (1, 0)])


def from_others(values, axes):
    count = lax.axis_size(axes)
    return [
        lax.ppermute(values, axes, [(i, (i + step) % count) for i in range(count)])
        for step in range(1, count)
    ]


def near_exchange(values):
    return lax.all_to_all(values, NEAR, 0, 0, tiled=True)


def far_sum(sent):
    one, two, three = [block.astype(F32) for block in from_others(sent, FAR)]
    return (sent.astype(F32) + two) + (one + three)


def near_gather(values):
    count = lax.axis_size(NEAR)
    sent = jnp.broadcast_to(values[None], (count,) + values.shape)
    return near_exchange(sent).reshape(-1, values.shape[-1])


def on_device(peak_bins, peak_values, enc_weight, enc_bias, dec_weight):
    width, hidden_size = enc_weight.shape
    core = lax.axis_index("core")
    group = lax.axis_index(SPECTRA_AXES)
    position = lax.axis_index(NAMES)
    stride = lax.axis_size(SPECTRA_AXES)
    partner = position + (1 - 2 * core) * stride
    place = jnp.stack([position * width, partner * width, group]).astype(jnp.int32)
    packed = pack_peaks(core.reshape(1), peak_bins, peak_values)
    enc_weights = (enc_weight, swap(enc_weight))
    dec_weights = (dec_weight, swap(dec_weight))
    dense_own, dense_pair = build_dense(
        place, [packed] + from_others(packed, SPECTRA_AXES), width
    )
    dense = (dense_own, dense_pair)
    dense_other = swap(dense_pair)

    def encode(block, weight):
        return jnp.dot(block, weight, preferred_element_type=F32)

    def residual(block, hidden, weight):
        recon = jnp.dot(hidden, weight, preferred_element_type=F32)
        return (recon - block.astype(F32)).astype(BF16)

    def decode_back(resid, weight):
        return lax.dot_general(
            resid, weight, (((1,), (1,)), ((), ())), preferred_element_type=F32
        )

    def rows_dot(left, right):
        return lax.dot_general(
            left, right, (((0,), (0,)), ((), ())), preferred_element_type=F32
        )

    def near_parts(rows):
        return near_exchange(rows.astype(BF16).reshape(lax.axis_size(NEAR), -1, hidden_size))

    parts = near_parts(sum(map(encode, dense, enc_weights)))
    pre = far_sum(sum_parts(parts)) + enc_bias
    hidden = near_gather(activation(pre).astype(BF16))
    resid = [residual(block, hidden, weight) for block, weight in zip(dense, dec_weights)]
    parts = near_parts(sum(map(decode_back, resid, dec_weights)))
    grad_dec = rows_dot(
        jnp.concatenate([hidden, swap(hidden)]), jnp.concatenate([resid[0], swap(resid[1])])
    ).astype(BF16)
    parts, grad_dec, dense_other = lax.optimization_barrier((parts, grad_dec, dense_other))
    back = far_sum(sum_parts(parts))
    dpre = near_gather(slope_times(pre, back))
    grad_own, dpre_other = lax.optimization_barrier((rows_dot(dense_own, dpre), swap(dpre)))
    grad_enc = (grad_own + rows_dot(dense_other, dpre_other)).astype(BF16)
    return (grad_enc, grad_dec)


def solution(mesh):
    fine = Mesh(mesh.devices.reshape(SHAPE), NAMES)
    placed = (
        P(SPECTRA_AXES, None),
        P(SPECTRA_AXES, None),
        P(NAMES, None),
        P(),
        P(None, NAMES),
    )
    return jax.shard_map(
        on_device,
        mesh=fine,
        in_specs=placed,
        out_specs=(P(NAMES, None), P(None, NAMES)),
        check_vma=False,
    )
```

```python
import functools

import jax
import jax.numpy as jnp
from jax import lax
from jax.experimental import pallas as pl
from jax.experimental.pallas import tpu as pltpu
from jax.sharding import Mesh
from jax.sharding import PartitionSpec as P

SHAPE = (4, 2, 4, 2, 2, 2)
NAMES = ("x", "zhi", "y", "core", "zp", "zq")
NEAR = ("x", "y", "zq")
FAR = ("zhi", "zp")
SPECTRA_AXES = ("zp", "zq")
DEPTH = ("zhi", "zp", "zq")
LANES = 128
STEP = 512
CHUNK = 512
BF16 = jnp.bfloat16
F32 = jnp.float32
SMEM_SPEC = pl.BlockSpec(memory_space=pltpu.SMEM)
VMEM_SPEC = pl.BlockSpec(memory_space=pltpu.VMEM)
HBM_SPEC = pl.BlockSpec(memory_space=pltpu.HBM)


def activation(values):
    return jax.nn.gelu(values, approximate=True)


def slope_times(pre, back):
    _, pullback = jax.vjp(activation, pre)
    return pullback(back)[0].astype(BF16)


def pack_kernel(core_ref, bins_ref, values_ref, out_hbm, out_ref, sem):
    rows, lanes = out_ref.shape
    peaks = lanes // 3
    first = pl.multiple_of(core_ref[0] * rows, rows)
    bins = bins_ref[pl.ds(first, rows), :]
    out_ref[:, :peaks] = ((bins >> 9) - 192).astype(F32).astype(BF16)
    out_ref[:, peaks : 2 * peaks] = ((bins & (STEP - 1)) - 256).astype(F32).astype(BF16)
    out_ref[:, 2 * peaks :] = values_ref[pl.ds(first, rows), :]
    copy = pltpu.make_async_copy(out_ref, out_hbm, sem)
    copy.start()
    copy.wait()


def pack_peaks(core, bins, values):
    rows, peaks = bins.shape
    packed = (rows // 2, 3 * peaks)
    whole = pl.BlockSpec(bins.shape, lambda i: (0, 0))
    return pl.pallas_call(
        pack_kernel,
        out_shape=jax.ShapeDtypeStruct(packed, BF16),
        grid=(1,),
        in_specs=[SMEM_SPEC, whole, whole],
        out_specs=HBM_SPEC,
        scratch_shapes=[pltpu.VMEM(packed, BF16), pltpu.SemaphoreType.DMA],
        compiler_params=pltpu.CompilerParams(vmem_limit_bytes=4 << 20),
        name="pack_peaks",
    )(core, bins, values)


def dense_rows(bins, values, firsts, tiles, consts):
    lane, upper, which = consts
    low = (bins & (LANES - 1)).astype(BF16)
    twice = jnp.concatenate([values, values], axis=0).astype(BF16)
    picked = []
    for first in firsts:
        local = bins - first
        inside = (local >= 0) & (local < tiles * LANES)
        high = jnp.where(inside, local >> 7, -9).astype(F32)
        high = jnp.concatenate([high, high], axis=0).astype(BF16) - upper
        for tile in range(0, tiles, 2):
            picked.append(jnp.where(high == tile, twice, jnp.zeros_like(twice)))
    left = jnp.concatenate(
        [
            jnp.concatenate(
                [jnp.where(which == row, one, jnp.zeros_like(one)) for one in picked], axis=0
            )
            for row in range(8)
        ],
        axis=1,
    )
    ones = jnp.ones((LANES, LANES), BF16)
    right = jnp.concatenate(
        [jnp.where(low[row][None, :] == lane, ones, jnp.zeros_like(ones)) for row in range(8)],
        axis=1,
    )
    return lax.dot_general(left, right, (((1,), (1,)), ((), ())), preferred_element_type=F32)


def encode_kernel(place_ref, *refs, groups):
    packed_hbm, weight_hbm = refs[:groups], refs[groups : groups + 2]
    own_hbm, pair_hbm, rows_hbm = refs[groups + 2 : groups + 5]
    packed_refs, weight_refs, own_ref, pair_ref, rows_ref, sems = refs[groups + 5 :]
    packed_in = [
        pltpu.make_async_copy(packed_hbm[k], packed_refs.at[k], sems.at[k]) for k in range(groups)
    ]
    weight_in = [
        pltpu.make_async_copy(weight_hbm[k], weight_refs.at[k], sems.at[groups + k])
        for k in range(2)
    ]
    for copy in packed_in + weight_in:
        copy.start()
    _, rows, lanes = packed_refs.shape
    peaks = lanes // 3
    tiles = own_ref.shape[1] // LANES
    firsts = (place_ref[0], place_ref[1])
    lane = lax.broadcasted_iota(jnp.int32, (LANES, 1), 0).astype(BF16)
    row16 = lax.broadcasted_iota(jnp.int32, (16, LANES), 0)
    consts = (lane, (row16 >= 8).astype(jnp.int32).astype(BF16), (row16 & 7).astype(BF16))
    for back in range(groups):
        base = lax.rem(place_ref[2] + groups - back, groups) * rows
        packed_in[back].wait()

        def step(group, carry, back=back, base=base):
            row = pl.multiple_of(group * 16, 16)
            block = packed_refs[back, pl.ds(row, 16), :].astype(F32)
            bins = (block[:, :peaks].astype(jnp.int32) + 192) * STEP
            bins = bins + block[:, peaks : 2 * peaks].astype(jnp.int32) + 256
            values = block[:, 2 * peaks :]
            sums = [
                dense_rows(bins[h : h + 8], values[h : h + 8], firsts, tiles, consts)
                for h in (0, 8)
            ]
            target = pl.multiple_of(base + row, 16)
            for ref, skip in ((own_ref, 0), (pair_ref, tiles)):
                for tile in range(tiles):
                    at = (skip + tile) * 8
                    ref[pl.ds(target, 16), tile * LANES : (tile + 1) * LANES] = jnp.concatenate(
                        [one[at : at + 8] for one in sums], axis=0
                    ).astype(BF16)
            return carry

        lax.fori_loop(0, rows // 16, step, 0, unroll=True)
    out = [
        pltpu.make_async_copy(own_ref, own_hbm, sems.at[groups + 2]),
        pltpu.make_async_copy(pair_ref, pair_hbm, sems.at[groups + 3]),
    ]
    for copy in out:
        copy.start()
    for copy in weight_in:
        copy.wait()
    parts, part_rows, columns = rows_ref.shape
    for first in range(0, columns, CHUNK):
        at = slice(first, first + CHUNK)
        total = jnp.dot(own_ref[...], weight_refs[0, :, at], preferred_element_type=F32)
        total += jnp.dot(pair_ref[...], weight_refs[1, :, at], preferred_element_type=F32)
        rows_ref[:, :, at] = total.reshape(parts, part_rows, CHUNK).astype(BF16)
        copy = pltpu.make_async_copy(
            rows_ref.at[:, :, pl.ds(first, CHUNK)],
            rows_hbm.at[:, :, pl.ds(first, CHUNK)],
            sems.at[groups + 4 + first // CHUNK],
        )
        copy.start()
        out.append(copy)
    for copy in out:
        copy.wait()


def encode_rows(place, blocks, weights, parts):
    width, columns = weights[0].shape
    groups = len(blocks)
    rows = blocks[0].shape[0] * groups
    dense = jax.ShapeDtypeStruct((rows, width), BF16)
    product = (parts, rows // parts, columns)
    return pl.pallas_call(
        functools.partial(encode_kernel, groups=groups),
        out_shape=(dense, dense, jax.ShapeDtypeStruct(product, BF16)),
        in_specs=[SMEM_SPEC] + [HBM_SPEC] * (groups + 2),
        out_specs=(HBM_SPEC,) * 3,
        scratch_shapes=[
            pltpu.VMEM((groups,) + blocks[0].shape, BF16),
            pltpu.VMEM((2, width, columns), BF16),
            pltpu.VMEM((rows, width), BF16),
            pltpu.VMEM((rows, width), BF16),
            pltpu.VMEM(product, BF16),
            pltpu.SemaphoreType.DMA((groups + 4 + columns // CHUNK,)),
        ],
        compiler_params=pltpu.CompilerParams(vmem_limit_bytes=50 << 20),
        name="encode_rows",
    )(place, *blocks, *weights)


def decode_kernel(hidden_ref, own_hbm, pair_hbm, own_w, pair_w, own_out, pair_out, rows_hbm, *scratch):
    weight_refs, dense_refs, resid_refs, total_ref, rows_ref, sems, out_sems = scratch
    chunks, hidden_size, block = weight_refs.shape
    half = chunks // 2
    dense_in = [
        pltpu.make_async_copy(source, dense_refs.at[k], sems.at[chunks + k])
        for k, source in enumerate((own_hbm, pair_hbm))
    ]
    copies = []
    for chunk in range(chunks):
        source = own_w if chunk < half else pair_w
        at = pl.ds((chunk % half) * block, block)
        copies.append(
            pltpu.make_async_copy(source.at[:, at], weight_refs.at[chunk], sems.at[chunk])
        )
    for copy in copies[:1] + dense_in + copies[1:]:
        copy.start()
    parts, part_rows, _ = rows_ref.shape
    hidden = hidden_ref[...].reshape(parts * part_rows, hidden_size)
    out = []
    for chunk in range(chunks):
        side = chunk // half
        at = slice((chunk % half) * block, (chunk % half + 1) * block)
        copies[chunk].wait()
        recon = jnp.dot(hidden, weight_refs[chunk], preferred_element_type=F32)
        if chunk % half == 0:
            dense_in[side].wait()
        resid = (recon - dense_refs[side, :, at].astype(F32)).astype(BF16)
        resid_refs[side, :, at] = resid
        if chunk % half == half - 1:
            copy = pltpu.make_async_copy(
                resid_refs.at[side], (own_out, pair_out)[side], out_sems.at[side]
            )
            copy.start()
            out.append(copy)
        for first in range(0, hidden_size, CHUNK):
            to = slice(first, first + CHUNK)
            term = lax.dot_general(
                resid,
                weight_refs[chunk, to, :],
                (((1,), (1,)), ((), ())),
                preferred_element_type=F32,
            )
            if chunk == 0:
                total_ref[:, to] = term
            elif chunk < chunks - 1:
                total_ref[:, to] += term
            else:
                total = total_ref[:, to] + term
                rows_ref[:, :, to] = total.reshape(parts, part_rows, CHUNK).astype(BF16)
                copy = pltpu.make_async_copy(
                    rows_ref.at[:, :, pl.ds(first, CHUNK)],
                    rows_hbm.at[:, :, pl.ds(first, CHUNK)],
                    out_sems.at[2 + first // CHUNK],
                )
                copy.start()
                out.append(copy)
    for copy in out:
        copy.wait()


def decode_rows(hidden, dense, weights):
    _, _, hidden_size = hidden.shape
    rows, width = dense[0].shape
    resid = jax.ShapeDtypeStruct((rows, width), BF16)
    block = 2 * LANES
    chunks = 2 * width // block
    return pl.pallas_call(
        decode_kernel,
        out_shape=(resid, resid, jax.ShapeDtypeStruct(hidden.shape, BF16)),
        in_specs=[VMEM_SPEC] + [HBM_SPEC] * 4,
        out_specs=(HBM_SPEC,) * 3,
        scratch_shapes=[
            pltpu.VMEM((chunks, hidden_size, block), BF16),
            pltpu.VMEM((2, rows, width), BF16),
            pltpu.VMEM((2, rows, width), BF16),
            pltpu.VMEM((rows, hidden_size), F32),
            pltpu.VMEM(hidden.shape, BF16),
            pltpu.SemaphoreType.DMA((chunks + 2,)),
            pltpu.SemaphoreType.DMA((2 + hidden_size // CHUNK,)),
        ],
        compiler_params=pltpu.CompilerParams(vmem_limit_bytes=50 << 20),
        name="decode_rows",
    )(hidden, *dense, *weights)


def weight_grad_kernel(own_ref, other_ref, left_ref, right_ref, out_ref):
    total = lax.dot_general(
        own_ref[...], left_ref[...], (((0,), (0,)), ((), ())), preferred_element_type=F32
    )
    total += lax.dot_general(
        other_ref[...], right_ref[...], (((0,), (0,)), ((), ())), preferred_element_type=F32
    )
    out_ref[...] = total.astype(BF16)


def weight_grad(own, other, left, right):
    rows, width = own.shape
    columns = left.shape[1]
    block = pl.BlockSpec((rows, LANES), lambda i: (0, i))
    return pl.pallas_call(
        weight_grad_kernel,
        out_shape=jax.ShapeDtypeStruct((width, columns), BF16),
        grid=(width // LANES,),
        in_specs=[block, block, VMEM_SPEC, VMEM_SPEC],
        out_specs=pl.BlockSpec((LANES, columns), lambda i: (i, 0)),
        compiler_params=pltpu.CompilerParams(vmem_limit_bytes=16 << 20),
        name="weight_grad",
    )(own, other, left, right)


def sum_kernel(parts_ref, out_ref):
    count, _, columns = parts_ref.shape
    block = 4 * LANES
    for first in range(0, columns, block):
        at = slice(first, first + block)
        total = parts_ref[0, :, at].astype(F32)
        for part in range(1, count):
            total = total + parts_ref[part, :, at].astype(F32)
        out_ref[:, at] = total.astype(out_ref.dtype)


def sum_parts(parts):
    return pl.pallas_call(
        sum_kernel,
        out_shape=jax.ShapeDtypeStruct(parts.shape[1:], BF16),
        in_specs=[VMEM_SPEC],
        out_specs=VMEM_SPEC,
        compiler_params=pltpu.CompilerParams(vmem_limit_bytes=4 << 20),
        name="sum_parts",
    )(parts)


def swap(values):
    return lax.ppermute(values, "core", [(0, 1), (1, 0)])


def from_others(values, axes, steps):
    count = lax.axis_size(axes)
    return [
        lax.ppermute(values, axes, [(i, (i + step) % count) for i in range(count)])
        for step in steps
    ]


def near_exchange(values):
    return lax.all_to_all(values, NEAR, 0, 0, tiled=True)


def far_sum(sent):
    one, two, three = [block.astype(F32) for block in from_others(sent, FAR, (1, 2, 3))]
    return (sent.astype(F32) + two) + (one + three)


def near_gather(values):
    count = lax.axis_size(NEAR)
    sent = jnp.broadcast_to(values[None], (count,) + values.shape)
    return near_exchange(sent)


def on_device(peak_bins, peak_values, enc_weight, enc_bias, dec_weight):
    width, hidden_size = enc_weight.shape
    core = lax.axis_index("core")
    group = lax.axis_index(SPECTRA_AXES)
    position = lax.axis_index(NAMES)
    stride = lax.axis_size(SPECTRA_AXES)
    partner = position + (1 - 2 * core) * stride
    place = jnp.stack([position * width, partner * width, group]).astype(jnp.int32)
    packed = pack_peaks(core.reshape(1), peak_bins, peak_values)
    enc_weights = (enc_weight, swap(enc_weight))
    dec_weights = (dec_weight, swap(dec_weight))
    peaks = [packed] + from_others(packed, DEPTH, (1, 2, -1))
    dense_own, dense_pair, rows = encode_rows(place, peaks, enc_weights, lax.axis_size(NEAR))
    dense_other = swap(dense_pair)
    pre = far_sum(sum_parts(near_exchange(rows))) + enc_bias
    hidden = near_gather(activation(pre).astype(BF16))
    resid_own, resid_pair, rows = decode_rows(hidden, (dense_own, dense_pair), dec_weights)
    parts = near_exchange(rows)
    hidden = hidden.reshape(-1, hidden_size)
    grad_dec = lax.dot_general(
        jnp.concatenate([hidden, swap(hidden)]),
        jnp.concatenate([resid_own, swap(resid_pair)]),
        (((0,), (0,)), ((), ())),
        preferred_element_type=F32,
    ).astype(BF16)
    parts, grad_dec, dense_other = lax.optimization_barrier((parts, grad_dec, dense_other))
    back = far_sum(sum_parts(parts))
    dpre = near_gather(slope_times(pre, back)).reshape(-1, hidden_size)
    grad_enc = weight_grad(dense_own, dense_other, dpre, swap(dpre))
    return (grad_enc, grad_dec)


def solution(mesh):
    fine = Mesh(mesh.devices.reshape(SHAPE), NAMES)
    placed = (
        P(SPECTRA_AXES, None),
        P(SPECTRA_AXES, None),
        P(NAMES, None),
        P(),
        P(None, NAMES),
    )
    return jax.shard_map(
        on_device,
        mesh=fine,
        in_specs=placed,
        out_specs=(P(NAMES, None), P(None, NAMES)),
        check_vma=False,
    )
```

```python
import functools

import jax
import jax.numpy as jnp
from jax import lax
from jax.experimental import pallas as pl
from jax.experimental.pallas import tpu as pltpu
from jax.sharding import Mesh
from jax.sharding import PartitionSpec as P

SHAPE = (4, 2, 4, 2, 2, 2)
NAMES = ("x", "zhi", "y", "core", "zp", "zq")
NEAR = ("x", "y", "zq")
FAR = ("zhi", "zp")
SPECTRA_AXES = ("zp", "zq")
LANES = 128
STEP = 512
PACK_VMEM = 60 << 20
DENSE_VMEM = 8 << 20
BF16 = jnp.bfloat16
F32 = jnp.float32


def activation(values):
    return jax.nn.gelu(values, approximate=True)


def slope_times(pre, back):
    _, pullback = jax.vjp(activation, pre)
    return pullback(back)[0].astype(BF16)


def pack_kernel(core_ref, bins_ref, values_ref, out_ref):
    rows, lanes = out_ref.shape
    peaks = lanes // 3
    first = pl.multiple_of(core_ref[0] * rows, rows)
    bins = bins_ref[pl.ds(first, rows), :]
    out_ref[:, :peaks] = ((bins >> 9) - 192).astype(F32).astype(BF16)
    out_ref[:, peaks : 2 * peaks] = ((bins & (STEP - 1)) - 256).astype(F32).astype(BF16)
    out_ref[:, 2 * peaks :] = values_ref[pl.ds(first, rows), :]


def pack_peaks(core, bins, values):
    rows, peaks = bins.shape
    whole = pl.BlockSpec(bins.shape, lambda i: (0, 0))
    packed = (rows // 2, 3 * peaks)
    return pl.pallas_call(
        pack_kernel,
        out_shape=jax.ShapeDtypeStruct(packed, BF16),
        grid=(1,),
        in_specs=[pl.BlockSpec(memory_space=pltpu.SMEM), whole, whole],
        out_specs=pl.BlockSpec(packed, lambda i: (0, 0)),
        compiler_params=pltpu.CompilerParams(vmem_limit_bytes=PACK_VMEM),
        name="pack_peaks",
    )(core, bins, values)


def dense_rows(bins, values, firsts, tiles, consts):
    lane, upper, which = consts
    low = (bins & (LANES - 1)).astype(BF16)
    twice = jnp.concatenate([values, values], axis=0).astype(BF16)
    picked = []
    for first in firsts:
        local = bins - first
        inside = (local >= 0) & (local < tiles * LANES)
        high = jnp.where(inside, local >> 7, -9).astype(F32)
        high = jnp.concatenate([high, high], axis=0).astype(BF16) - upper
        for tile in range(0, tiles, 2):
            picked.append(jnp.where(high == tile, twice, jnp.zeros_like(twice)))
    left = jnp.concatenate(
        [
            jnp.concatenate(
                [jnp.where(which == row, one, jnp.zeros_like(one)) for one in picked], axis=0
            )
            for row in range(8)
        ],
        axis=1,
    )
    ones = jnp.ones((LANES, LANES), BF16)
    right = jnp.concatenate(
        [jnp.where(low[row][None, :] == lane, ones, jnp.zeros_like(ones)) for row in range(8)],
        axis=1,
    )
    return lax.dot_general(left, right, (((1,), (1,)), ((), ())), preferred_element_type=F32)


def dense_kernel(place_ref, packed_ref, *refs, back, groups):
    own_ref, pair_ref = refs[-2:]
    rows, lanes = packed_ref.shape
    peaks = lanes // 3
    tiles = own_ref.shape[1] // LANES
    firsts = (place_ref[0], place_ref[1])
    lane = lax.broadcasted_iota(jnp.int32, (LANES, 1), 0).astype(BF16)
    row16 = lax.broadcasted_iota(jnp.int32, (16, LANES), 0)
    consts = (lane, (row16 >= 8).astype(jnp.int32).astype(BF16), (row16 & 7).astype(BF16))
    base = lax.rem(place_ref[2] + groups - back, groups) * rows

    def step(group, carry):
        row = pl.multiple_of(group * 16, 16)
        block = packed_ref[pl.ds(row, 16), :].astype(F32)
        bins = (block[:, :peaks].astype(jnp.int32) + 192) * STEP
        bins = bins + block[:, peaks : 2 * peaks].astype(jnp.int32) + 256
        values = block[:, 2 * peaks :]
        sums = [
            dense_rows(bins[h : h + 8], values[h : h + 8], firsts, tiles, consts)
            for h in (0, 8)
        ]
        target = pl.multiple_of(base + row, 16)
        for ref, skip in ((own_ref, 0), (pair_ref, tiles)):
            for tile in range(tiles):
                at = (skip + tile) * 8
                ref[pl.ds(target, 16), tile * LANES : (tile + 1) * LANES] = jnp.concatenate(
                    [one[at : at + 8] for one in sums], axis=0
                ).astype(BF16)
        return carry

    lax.fori_loop(0, rows // 16, step, 0, unroll=True)


def build_dense(place, blocks, width):
    groups = len(blocks)
    part = blocks[0].shape
    rows = part[0] * groups
    vmem = pl.BlockSpec(memory_space=pltpu.VMEM)
    dense = ()
    for back, block in enumerate(blocks):
        dense = pl.pallas_call(
            functools.partial(dense_kernel, back=back, groups=groups),
            out_shape=(jax.ShapeDtypeStruct((rows, width), BF16),) * 2,
            grid=(1,),
            in_specs=[
                pl.BlockSpec(memory_space=pltpu.SMEM),
                pl.BlockSpec(part, lambda i: (0, 0)),
            ]
            + [vmem] * len(dense),
            out_specs=(vmem, vmem),
            input_output_aliases={2 + k: k for k in range(len(dense))},
            compiler_params=pltpu.CompilerParams(vmem_limit_bytes=DENSE_VMEM),
            cost_estimate=pl.CostEstimate(
                flops=1_000_000_000, bytes_accessed=3_000_000, transcendentals=0
            ),
            name="build_dense",
        )(place, block, *dense)
    return dense


def sum_kernel(parts_ref, out_ref):
    count, _, columns = parts_ref.shape
    block = 4 * LANES
    for first in range(0, columns, block):
        at = slice(first, first + block)
        total = parts_ref[0, :, at].astype(F32)
        for part in range(1, count):
            total = total + parts_ref[part, :, at].astype(F32)
        out_ref[:, at] = total.astype(out_ref.dtype)


def sum_parts(parts):
    vmem = pl.BlockSpec(memory_space=pltpu.VMEM)
    return pl.pallas_call(
        sum_kernel,
        out_shape=jax.ShapeDtypeStruct(parts.shape[1:], BF16),
        in_specs=[vmem],
        out_specs=vmem,
        compiler_params=pltpu.CompilerParams(vmem_limit_bytes=4 << 20),
        name="sum_parts",
    )(parts)


def swap(values):
    return lax.ppermute(values, "core", [(0, 1), (1, 0)])


def from_others(values, axes):
    count = lax.axis_size(axes)
    return [
        lax.ppermute(values, axes, [(i, (i + step) % count) for i in range(count)])
        for step in range(1, count)
    ]


def near_exchange(values):
    return lax.all_to_all(values, NEAR, 0, 0, tiled=True)


def far_sum(sent):
    one, two, three = [block.astype(F32) for block in from_others(sent, FAR)]
    return (sent.astype(F32) + two) + (one + three)


def near_gather(values):
    count = lax.axis_size(NEAR)
    sent = jnp.broadcast_to(values[None], (count,) + values.shape)
    return near_exchange(sent).reshape(-1, values.shape[-1])


def on_device(peak_bins, peak_values, enc_weight, enc_bias, dec_weight):
    width, hidden_size = enc_weight.shape
    core = lax.axis_index("core")
    group = lax.axis_index(SPECTRA_AXES)
    position = lax.axis_index(NAMES)
    stride = lax.axis_size(SPECTRA_AXES)
    partner = position + (1 - 2 * core) * stride
    place = jnp.stack([position * width, partner * width, group]).astype(jnp.int32)
    packed = pack_peaks(core.reshape(1), peak_bins, peak_values)
    enc_weights = (enc_weight, swap(enc_weight))
    dense_own, dense_pair = build_dense(
        place, [packed] + from_others(packed, SPECTRA_AXES), width
    )
    dense = (dense_own, dense_pair)
    dense_other = swap(dense_pair)

    def encode(block, weight):
        return jnp.dot(block, weight, preferred_element_type=F32)

    def residual(block, hidden, weight):
        recon = jnp.dot(hidden, weight, preferred_element_type=F32)
        return (recon - block.astype(F32)).astype(BF16)

    def decode_back(resid, weight):
        return lax.dot_general(
            resid, weight, (((1,), (1,)), ((), ())), preferred_element_type=F32
        )

    def rows_dot(left, right):
        return lax.dot_general(
            left, right, (((0,), (0,)), ((), ())), preferred_element_type=F32
        )

    def near_parts(rows):
        return near_exchange(rows.astype(BF16).reshape(lax.axis_size(NEAR), -1, hidden_size))

    parts = near_parts(sum(map(encode, dense, enc_weights)))
    parts, sent_weight = lax.optimization_barrier((parts, dec_weight))
    dec_weights = (dec_weight, swap(sent_weight))
    pre = far_sum(sum_parts(parts)) + enc_bias
    hidden = near_gather(activation(pre).astype(BF16))
    resid = lax.optimization_barrier(
        [residual(block, hidden, weight) for block, weight in zip(dense, dec_weights)]
    )
    parts = near_parts(sum(map(decode_back, resid, dec_weights)))
    grad_dec = rows_dot(
        jnp.concatenate([hidden, swap(hidden)]), jnp.concatenate([resid[0], swap(resid[1])])
    ).astype(BF16)
    parts, grad_dec, dense_other = lax.optimization_barrier((parts, grad_dec, dense_other))
    back = far_sum(sum_parts(parts))
    dpre = near_gather(slope_times(pre, back))
    grad_own = lax.optimization_barrier(rows_dot(dense_own, dpre))
    grad_enc = (rows_dot(dense_other, swap(dpre)) + grad_own).astype(BF16)
    return (grad_enc, grad_dec)


def solution(mesh):
    fine = Mesh(mesh.devices.reshape(SHAPE), NAMES)
    placed = (
        P(SPECTRA_AXES, None),
        P(SPECTRA_AXES, None),
        P(NAMES, None),
        P(),
        P(None, NAMES),
    )
    return jax.shard_map(
        on_device,
        mesh=fine,
        in_specs=placed,
        out_specs=(P(NAMES, None), P(None, NAMES)),
        check_vma=False,
    )
```

```python
import functools

import jax
import jax.numpy as jnp
from jax import lax
from jax.experimental import pallas as pl
from jax.experimental.pallas import tpu as pltpu
from jax.sharding import Mesh
from jax.sharding import PartitionSpec as P

SHAPE = (4, 2, 4, 2, 2, 2)
NAMES = ("x", "zhi", "y", "core", "zp", "zq")
NEAR = ("x", "y", "zq")
FAR = ("zhi", "zp")
SPECTRA_AXES = ("zp", "zq")
LANES = 128
STEP = 512
PACK_VMEM = 50 << 20
DENSE_VMEM = 8 << 20
BF16 = jnp.bfloat16
F32 = jnp.float32


def activation(values):
    return jax.nn.gelu(values, approximate=True)


def slope_times(pre, back):
    _, pullback = jax.vjp(activation, pre)
    return pullback(back)[0].astype(BF16)


def pack_kernel(core_ref, bins_ref, values_ref, out_ref):
    rows, lanes = out_ref.shape
    peaks = lanes // 3
    first = pl.multiple_of(core_ref[0] * rows, rows)
    bins = bins_ref[pl.ds(first, rows), :]
    out_ref[:, :peaks] = ((bins >> 9) - 192).astype(F32).astype(BF16)
    out_ref[:, peaks : 2 * peaks] = ((bins & (STEP - 1)) - 256).astype(F32).astype(BF16)
    out_ref[:, 2 * peaks :] = values_ref[pl.ds(first, rows), :]


def pack_peaks(core, bins, values):
    rows, peaks = bins.shape
    whole = pl.BlockSpec(bins.shape, lambda i: (0, 0))
    packed = (rows // 2, 3 * peaks)
    return pl.pallas_call(
        pack_kernel,
        out_shape=jax.ShapeDtypeStruct(packed, BF16),
        grid=(1,),
        in_specs=[pl.BlockSpec(memory_space=pltpu.SMEM), whole, whole],
        out_specs=pl.BlockSpec(memory_space=pltpu.VMEM),
        compiler_params=pltpu.CompilerParams(vmem_limit_bytes=PACK_VMEM),
        name="pack_peaks",
    )(core, bins, values)


def dense_rows(bins, values, firsts, tiles, consts):
    lane, upper, which = consts
    low = (bins & (LANES - 1)).astype(BF16)
    twice = jnp.concatenate([values, values], axis=0).astype(BF16)
    picked = []
    for first in firsts:
        local = bins - first
        inside = (local >= 0) & (local < tiles * LANES)
        high = jnp.where(inside, local >> 7, -9).astype(F32)
        high = jnp.concatenate([high, high], axis=0).astype(BF16) - upper
        for tile in range(0, tiles, 2):
            picked.append(jnp.where(high == tile, twice, jnp.zeros_like(twice)))
    left = jnp.concatenate(
        [
            jnp.concatenate(
                [jnp.where(which == row, one, jnp.zeros_like(one)) for one in picked], axis=0
            )
            for row in range(8)
        ],
        axis=1,
    )
    ones = jnp.ones((LANES, LANES), BF16)
    right = jnp.concatenate(
        [jnp.where(low[row][None, :] == lane, ones, jnp.zeros_like(ones)) for row in range(8)],
        axis=1,
    )
    return lax.dot_general(left, right, (((1,), (1,)), ((), ())), preferred_element_type=F32)


def dense_kernel(place_ref, *refs, backs, groups):
    packed_refs, (own_ref, pair_ref) = refs[: len(backs)], refs[-2:]
    rows, lanes = packed_refs[0].shape
    peaks = lanes // 3
    tiles = own_ref.shape[1] // LANES
    firsts = (place_ref[0], place_ref[1])
    lane = lax.broadcasted_iota(jnp.int32, (LANES, 1), 0).astype(BF16)
    row16 = lax.broadcasted_iota(jnp.int32, (16, LANES), 0)
    consts = (lane, (row16 >= 8).astype(jnp.int32).astype(BF16), (row16 & 7).astype(BF16))

    def step(group, carry, packed_ref, base):
        row = pl.multiple_of(group * 16, 16)
        block = packed_ref[pl.ds(row, 16), :].astype(F32)
        bins = (block[:, :peaks].astype(jnp.int32) + 192) * STEP
        bins = bins + block[:, peaks : 2 * peaks].astype(jnp.int32) + 256
        values = block[:, 2 * peaks :]
        sums = [
            dense_rows(bins[h : h + 8], values[h : h + 8], firsts, tiles, consts)
            for h in (0, 8)
        ]
        target = pl.multiple_of(base + row, 16)
        for ref, skip in ((own_ref, 0), (pair_ref, tiles)):
            for tile in range(tiles):
                at = (skip + tile) * 8
                ref[pl.ds(target, 16), tile * LANES : (tile + 1) * LANES] = jnp.concatenate(
                    [one[at : at + 8] for one in sums], axis=0
                ).astype(BF16)
        return carry

    for back, packed_ref in zip(backs, packed_refs):
        base = lax.rem(place_ref[2] + groups - back, groups) * rows
        block_step = functools.partial(step, packed_ref=packed_ref, base=base)
        lax.fori_loop(0, rows // 16, block_step, 0, unroll=True)


def build_dense(place, blocks, width):
    groups = len(blocks)
    part = blocks[0].shape
    rows = part[0] * groups
    vmem = pl.BlockSpec(memory_space=pltpu.VMEM)
    dense = ()
    for first in range(0, groups, 2):
        backs = (first, first + 1)
        dense = pl.pallas_call(
            functools.partial(dense_kernel, backs=backs, groups=groups),
            out_shape=(jax.ShapeDtypeStruct((rows, width), BF16),) * 2,
            grid=(1,),
            in_specs=[pl.BlockSpec(memory_space=pltpu.SMEM)]
            + [pl.BlockSpec(part, lambda i: (0, 0))] * 2
            + [vmem] * len(dense),
            out_specs=(vmem, vmem),
            input_output_aliases={3 + k: k for k in range(len(dense))},
            compiler_params=pltpu.CompilerParams(vmem_limit_bytes=DENSE_VMEM),
            cost_estimate=pl.CostEstimate(
                flops=1_000_000_000, bytes_accessed=3_000_000, transcendentals=0
            ),
            name="build_dense",
        )(place, *blocks[first : first + 2], *dense)
    return dense


def sum_kernel(parts_ref, out_ref):
    count, _, columns = parts_ref.shape
    block = 4 * LANES
    for first in range(0, columns, block):
        at = slice(first, first + block)
        total = parts_ref[0, :, at].astype(F32)
        for part in range(1, count):
            total = total + parts_ref[part, :, at].astype(F32)
        out_ref[:, at] = total.astype(out_ref.dtype)


def sum_parts(parts):
    vmem = pl.BlockSpec(memory_space=pltpu.VMEM)
    return pl.pallas_call(
        sum_kernel,
        out_shape=jax.ShapeDtypeStruct(parts.shape[1:], BF16),
        in_specs=[vmem],
        out_specs=vmem,
        compiler_params=pltpu.CompilerParams(vmem_limit_bytes=4 << 20),
        name="sum_parts",
    )(parts)


def swap(values):
    return lax.ppermute(values, "core", [(0, 1), (1, 0)])


def from_others(values, axes):
    count = lax.axis_size(axes)
    return [
        lax.ppermute(values, axes, [(i, (i + step) % count) for i in range(count)])
        for step in range(1, count)
    ]


def near_exchange(values):
    return lax.all_to_all(values, NEAR, 0, 0, tiled=True)


def copies_to(values, axes):
    count = lax.axis_size(axes)
    sent = jnp.broadcast_to(values[None], (count,) + values.shape)
    return lax.all_to_all(sent, axes, 0, 0, tiled=True)


def far_sum(values):
    blocks = copies_to(values, FAR).astype(F32)
    return (blocks[0] + blocks[1]) + (blocks[2] + blocks[3])


def near_gather(values):
    return copies_to(values, NEAR).reshape(-1, values.shape[-1])


def on_device(peak_bins, peak_values, enc_weight, enc_bias, dec_weight):
    width, hidden_size = enc_weight.shape
    core = lax.axis_index("core")
    group = lax.axis_index(SPECTRA_AXES)
    position = lax.axis_index(NAMES)
    stride = lax.axis_size(SPECTRA_AXES)
    partner = position + (1 - 2 * core) * stride
    place = jnp.stack([position * width, partner * width, group]).astype(jnp.int32)
    packed = pack_peaks(core.reshape(1), peak_bins, peak_values)
    enc_weights = (enc_weight, swap(enc_weight))
    dense_own, dense_pair = build_dense(
        place, [packed] + from_others(packed, SPECTRA_AXES), width
    )
    dense = (dense_own, dense_pair)
    dense_other = swap(dense_pair)

    def encode(block, weight):
        return jnp.dot(block, weight, preferred_element_type=F32)

    def residual(block, hidden, weight):
        recon = jnp.dot(hidden, weight, preferred_element_type=F32)
        return (recon - block.astype(F32)).astype(BF16)

    def decode_back(resid, weight):
        return lax.dot_general(
            resid, weight, (((1,), (1,)), ((), ())), preferred_element_type=F32
        )

    def rows_dot(left, right):
        return lax.dot_general(
            left, right, (((0,), (0,)), ((), ())), preferred_element_type=F32
        )

    def near_parts(rows):
        return near_exchange(rows.astype(BF16).reshape(lax.axis_size(NEAR), -1, hidden_size))

    parts = near_parts(sum(map(encode, dense, enc_weights)))
    parts, sent_weight = lax.optimization_barrier((parts, dec_weight))
    dec_weights = (dec_weight, swap(sent_weight))
    pre = far_sum(sum_parts(parts)) + enc_bias
    hidden = near_gather(activation(pre).astype(BF16))
    resid = lax.optimization_barrier(
        [residual(block, hidden, weight) for block, weight in zip(dense, dec_weights)]
    )
    parts = near_parts(sum(map(decode_back, resid, dec_weights)))
    grad_dec = rows_dot(
        jnp.concatenate([hidden, swap(hidden)]), jnp.concatenate([resid[0], swap(resid[1])])
    ).astype(BF16)
    parts, grad_dec, dense_other = lax.optimization_barrier((parts, grad_dec, dense_other))
    back = far_sum(sum_parts(parts))
    dpre = near_gather(slope_times(pre, back))
    grad_own = lax.optimization_barrier(rows_dot(dense_own, dpre))
    grad_enc = (rows_dot(dense_other, swap(dpre)) + grad_own).astype(BF16)
    return (grad_enc, grad_dec)


def solution(mesh):
    fine = Mesh(mesh.devices.reshape(SHAPE), NAMES)
    placed = (
        P(SPECTRA_AXES, None),
        P(SPECTRA_AXES, None),
        P(NAMES, None),
        P(),
        P(None, NAMES),
    )
    return jax.shard_map(
        on_device,
        mesh=fine,
        in_specs=placed,
        out_specs=(P(NAMES, None), P(None, NAMES)),
        check_vma=False,
    )
```

```python
import functools

import jax
import jax.numpy as jnp
from jax import lax
from jax.experimental import pallas as pl
from jax.experimental.pallas import tpu as pltpu
from jax.sharding import Mesh
from jax.sharding import PartitionSpec as P

SHAPE = (4, 2, 4, 2, 2, 2)
NAMES = ("x", "zhi", "y", "core", "zp", "zq")
NEAR = ("x", "y", "zq")
FAR = ("zhi", "zp")
SPECTRA_AXES = ("zp", "zq")
LANES = 128
STEP = 512
PACK_VMEM = 60 << 20
DENSE_VMEM = 8 << 20
BF16 = jnp.bfloat16
F32 = jnp.float32


def activation(values):
    return jax.nn.gelu(values, approximate=True)


def slope_times(pre, back):
    _, pullback = jax.vjp(activation, pre)
    return pullback(back)[0].astype(BF16)


def pack_kernel(core_ref, bins_ref, values_ref, out_ref):
    rows, lanes = out_ref.shape
    peaks = lanes // 3
    first = pl.multiple_of(core_ref[0] * rows, rows)
    bins = bins_ref[pl.ds(first, rows), :]
    out_ref[:, :peaks] = ((bins >> 9) - 192).astype(F32).astype(BF16)
    out_ref[:, peaks : 2 * peaks] = ((bins & (STEP - 1)) - 256).astype(F32).astype(BF16)
    out_ref[:, 2 * peaks :] = values_ref[pl.ds(first, rows), :]


def pack_peaks(core, bins, values):
    rows, peaks = bins.shape
    whole = pl.BlockSpec(bins.shape, lambda i: (0, 0))
    packed = (rows // 2, 3 * peaks)
    return pl.pallas_call(
        pack_kernel,
        out_shape=jax.ShapeDtypeStruct(packed, BF16),
        grid=(1,),
        in_specs=[pl.BlockSpec(memory_space=pltpu.SMEM), whole, whole],
        out_specs=pl.BlockSpec(packed, lambda i: (0, 0)),
        compiler_params=pltpu.CompilerParams(vmem_limit_bytes=PACK_VMEM),
        name="pack_peaks",
    )(core, bins, values)


def dense_rows(bins, values, firsts, tiles, consts):
    lane, upper, which = consts
    low = (bins & (LANES - 1)).astype(BF16)
    twice = jnp.concatenate([values, values], axis=0).astype(BF16)
    picked = []
    for first in firsts:
        local = bins - first
        inside = (local >= 0) & (local < tiles * LANES)
        high = jnp.where(inside, local >> 7, -9).astype(F32)
        high = jnp.concatenate([high, high], axis=0).astype(BF16) - upper
        for tile in range(0, tiles, 2):
            picked.append(jnp.where(high == tile, twice, jnp.zeros_like(twice)))
    left = jnp.concatenate(
        [
            jnp.concatenate(
                [jnp.where(which == row, one, jnp.zeros_like(one)) for one in picked], axis=0
            )
            for row in range(8)
        ],
        axis=1,
    )
    ones = jnp.ones((LANES, LANES), BF16)
    right = jnp.concatenate(
        [jnp.where(low[row][None, :] == lane, ones, jnp.zeros_like(ones)) for row in range(8)],
        axis=1,
    )
    return lax.dot_general(left, right, (((1,), (1,)), ((), ())), preferred_element_type=F32)


def dense_kernel(place_ref, packed_ref, *refs, back, groups):
    own_ref, pair_ref = refs[-2:]
    rows, lanes = packed_ref.shape
    peaks = lanes // 3
    tiles = own_ref.shape[1] // LANES
    firsts = (place_ref[0], place_ref[1])
    lane = lax.broadcasted_iota(jnp.int32, (LANES, 1), 0).astype(BF16)
    row16 = lax.broadcasted_iota(jnp.int32, (16, LANES), 0)
    consts = (lane, (row16 >= 8).astype(jnp.int32).astype(BF16), (row16 & 7).astype(BF16))
    base = lax.rem(place_ref[2] + groups - back, groups) * rows

    def step(group, carry):
        row = pl.multiple_of(group * 16, 16)
        block = packed_ref[pl.ds(row, 16), :].astype(F32)
        bins = (block[:, :peaks].astype(jnp.int32) + 192) * STEP
        bins = bins + block[:, peaks : 2 * peaks].astype(jnp.int32) + 256
        values = block[:, 2 * peaks :]
        sums = [
            dense_rows(bins[h : h + 8], values[h : h + 8], firsts, tiles, consts)
            for h in (0, 8)
        ]
        target = pl.multiple_of(base + row, 16)
        for ref, skip in ((own_ref, 0), (pair_ref, tiles)):
            for tile in range(tiles):
                at = (skip + tile) * 8
                ref[pl.ds(target, 16), tile * LANES : (tile + 1) * LANES] = jnp.concatenate(
                    [one[at : at + 8] for one in sums], axis=0
                ).astype(BF16)
        return carry

    lax.fori_loop(0, rows // 16, step, 0, unroll=True)


def build_dense(place, blocks, width):
    groups = len(blocks)
    part = blocks[0].shape
    rows = part[0] * groups
    vmem = pl.BlockSpec(memory_space=pltpu.VMEM)
    dense = ()
    for back, block in enumerate(blocks):
        dense = pl.pallas_call(
            functools.partial(dense_kernel, back=back, groups=groups),
            out_shape=(jax.ShapeDtypeStruct((rows, width), BF16),) * 2,
            grid=(1,),
            in_specs=[
                pl.BlockSpec(memory_space=pltpu.SMEM),
                pl.BlockSpec(part, lambda i: (0, 0)),
            ]
            + [vmem] * len(dense),
            out_specs=(vmem, vmem),
            input_output_aliases={2 + k: k for k in range(len(dense))},
            compiler_params=pltpu.CompilerParams(vmem_limit_bytes=DENSE_VMEM),
            cost_estimate=pl.CostEstimate(
                flops=1_000_000_000, bytes_accessed=3_000_000, transcendentals=0
            ),
            name="build_dense",
        )(place, block, *dense)
    return dense


def sum_kernel(parts_ref, out_ref):
    count, _, columns = parts_ref.shape
    block = 4 * LANES
    for first in range(0, columns, block):
        at = slice(first, first + block)
        total = parts_ref[0, :, at].astype(F32)
        for part in range(1, count):
            total = total + parts_ref[part, :, at].astype(F32)
        out_ref[:, at] = total.astype(out_ref.dtype)


def sum_parts(parts):
    vmem = pl.BlockSpec(memory_space=pltpu.VMEM)
    return pl.pallas_call(
        sum_kernel,
        out_shape=jax.ShapeDtypeStruct(parts.shape[1:], BF16),
        in_specs=[vmem],
        out_specs=vmem,
        compiler_params=pltpu.CompilerParams(vmem_limit_bytes=4 << 20),
        name="sum_parts",
    )(parts)


def swap(values):
    return lax.ppermute(values, "core", [(0, 1), (1, 0)])


def from_others(values, axes):
    count = lax.axis_size(axes)
    return [
        lax.ppermute(values, axes, [(i, (i + step) % count) for i in range(count)])
        for step in range(1, count)
    ]


def near_exchange(values):
    return lax.all_to_all(values, NEAR, 0, 0, tiled=True)


def far_sum(sent):
    one, two, three = [block.astype(F32) for block in from_others(sent, FAR)]
    return (sent.astype(F32) + two) + (one + three)


def near_gather(values):
    count = lax.axis_size(NEAR)
    sent = jnp.broadcast_to(values[None], (count,) + values.shape)
    return near_exchange(sent).reshape(-1, values.shape[-1])


def on_device(peak_bins, peak_values, enc_weight, enc_bias, dec_weight):
    width, hidden_size = enc_weight.shape
    core = lax.axis_index("core")
    group = lax.axis_index(SPECTRA_AXES)
    position = lax.axis_index(NAMES)
    stride = lax.axis_size(SPECTRA_AXES)
    partner = position + (1 - 2 * core) * stride
    place = jnp.stack([position * width, partner * width, group]).astype(jnp.int32)
    packed = pack_peaks(core.reshape(1), peak_bins, peak_values)
    enc_weights = (enc_weight, swap(enc_weight))
    dec_weights = (dec_weight, swap(dec_weight))
    dense_own, dense_pair = build_dense(
        place, [packed] + from_others(packed, SPECTRA_AXES), width
    )
    dense = (dense_own, dense_pair)
    dense_other = swap(dense_pair)

    def encode(block, weight):
        return jnp.dot(block, weight, preferred_element_type=F32)

    def residual(block, hidden, weight):
        recon = jnp.dot(hidden, weight, preferred_element_type=F32)
        return (recon - block.astype(F32)).astype(BF16)

    def decode_back(resid, weight):
        return lax.dot_general(
            resid, weight, (((1,), (1,)), ((), ())), preferred_element_type=F32
        )

    def rows_dot(left, right):
        return lax.dot_general(
            left, right, (((0,), (0,)), ((), ())), preferred_element_type=F32
        )

    def near_parts(rows):
        return near_exchange(rows.astype(BF16).reshape(lax.axis_size(NEAR), -1, hidden_size))

    parts = near_parts(sum(map(encode, dense, enc_weights)))
    pre = far_sum(sum_parts(parts)) + enc_bias
    hidden = near_gather(activation(pre).astype(BF16))
    resid = [
        lax.optimization_barrier(residual(block, hidden, weight))
        for block, weight in zip(dense, dec_weights)
    ]
    parts = near_parts(sum(map(decode_back, resid, dec_weights)))
    grad_dec = rows_dot(
        jnp.concatenate([hidden, swap(hidden)]), jnp.concatenate([resid[0], swap(resid[1])])
    ).astype(BF16)
    parts, grad_dec, dense_other = lax.optimization_barrier((parts, grad_dec, dense_other))
    back = far_sum(sum_parts(parts))
    dpre = near_gather(slope_times(pre, back))
    grad_own = lax.optimization_barrier(rows_dot(dense_own, dpre))
    grad_enc = (rows_dot(dense_other, swap(dpre)) + grad_own).astype(BF16)
    return (grad_enc, grad_dec)


def solution(mesh):
    fine = Mesh(mesh.devices.reshape(SHAPE), NAMES)
    placed = (
        P(SPECTRA_AXES, None),
        P(SPECTRA_AXES, None),
        P(NAMES, None),
        P(),
        P(None, NAMES),
    )
    return jax.shard_map(
        on_device,
        mesh=fine,
        in_specs=placed,
        out_specs=(P(NAMES, None), P(None, NAMES)),
        check_vma=False,
    )
```

```python
import functools

import jax
import jax.numpy as jnp
from jax import lax
from jax.experimental import pallas as pl
from jax.experimental.pallas import tpu as pltpu
from jax.sharding import Mesh
from jax.sharding import PartitionSpec as P

SHAPE = (4, 2, 4, 2, 2, 2)
NAMES = ("x", "zhi", "y", "core", "zp", "zq")
NEAR = ("x", "y", "zq")
FAR = ("zhi", "zp")
SPECTRA_AXES = ("zp", "zq")
LANES = 128
STEP = 512
PACK_VMEM = 60 << 20
DENSE_VMEM = 8 << 20
BF16 = jnp.bfloat16
F32 = jnp.float32


def activation(values):
    return jax.nn.gelu(values, approximate=True)


def slope_times(pre, back):
    _, pullback = jax.vjp(activation, pre)
    return pullback(back)[0].astype(BF16)


def pack_kernel(core_ref, bins_ref, values_ref, out_ref):
    rows, lanes = out_ref.shape
    peaks = lanes // 3
    first = pl.multiple_of(core_ref[0] * rows, rows)
    bins = bins_ref[pl.ds(first, rows), :]
    out_ref[:, :peaks] = ((bins >> 9) - 192).astype(F32).astype(BF16)
    out_ref[:, peaks : 2 * peaks] = ((bins & (STEP - 1)) - 256).astype(F32).astype(BF16)
    out_ref[:, 2 * peaks :] = values_ref[pl.ds(first, rows), :]


def pack_peaks(core, bins, values):
    rows, peaks = bins.shape
    whole = pl.BlockSpec(bins.shape, lambda i: (0, 0))
    packed = (rows // 2, 3 * peaks)
    return pl.pallas_call(
        pack_kernel,
        out_shape=jax.ShapeDtypeStruct(packed, BF16),
        grid=(1,),
        in_specs=[pl.BlockSpec(memory_space=pltpu.SMEM), whole, whole],
        out_specs=pl.BlockSpec(packed, lambda i: (0, 0)),
        compiler_params=pltpu.CompilerParams(vmem_limit_bytes=PACK_VMEM),
        name="pack_peaks",
    )(core, bins, values)


def dense_rows(bins, values, firsts, tiles, consts):
    lane, upper, which = consts
    low = (bins & (LANES - 1)).astype(BF16)
    twice = jnp.concatenate([values, values], axis=0).astype(BF16)
    picked = []
    for first in firsts:
        local = bins - first
        inside = (local >= 0) & (local < tiles * LANES)
        high = jnp.where(inside, local >> 7, -9).astype(F32)
        high = jnp.concatenate([high, high], axis=0).astype(BF16) - upper
        for tile in range(0, tiles, 2):
            picked.append(jnp.where(high == tile, twice, jnp.zeros_like(twice)))
    left = jnp.concatenate(
        [
            jnp.concatenate(
                [jnp.where(which == row, one, jnp.zeros_like(one)) for one in picked], axis=0
            )
            for row in range(8)
        ],
        axis=1,
    )
    ones = jnp.ones((LANES, LANES), BF16)
    right = jnp.concatenate(
        [jnp.where(low[row][None, :] == lane, ones, jnp.zeros_like(ones)) for row in range(8)],
        axis=1,
    )
    return lax.dot_general(left, right, (((1,), (1,)), ((), ())), preferred_element_type=F32)


def dense_kernel(place_ref, packed_ref, *refs, back, groups):
    own_ref, pair_ref = refs[-2:]
    rows, lanes = packed_ref.shape
    peaks = lanes // 3
    tiles = own_ref.shape[1] // LANES
    firsts = (place_ref[0], place_ref[1])
    lane = lax.broadcasted_iota(jnp.int32, (LANES, 1), 0).astype(BF16)
    row16 = lax.broadcasted_iota(jnp.int32, (16, LANES), 0)
    consts = (lane, (row16 >= 8).astype(jnp.int32).astype(BF16), (row16 & 7).astype(BF16))
    base = lax.rem(place_ref[2] + groups - back, groups) * rows

    def step(group, carry):
        row = pl.multiple_of(group * 16, 16)
        block = packed_ref[pl.ds(row, 16), :].astype(F32)
        bins = (block[:, :peaks].astype(jnp.int32) + 192) * STEP
        bins = bins + block[:, peaks : 2 * peaks].astype(jnp.int32) + 256
        values = block[:, 2 * peaks :]
        sums = [
            dense_rows(bins[h : h + 8], values[h : h + 8], firsts, tiles, consts)
            for h in (0, 8)
        ]
        target = pl.multiple_of(base + row, 16)
        for ref, skip in ((own_ref, 0), (pair_ref, tiles)):
            for tile in range(tiles):
                at = (skip + tile) * 8
                ref[pl.ds(target, 16), tile * LANES : (tile + 1) * LANES] = jnp.concatenate(
                    [one[at : at + 8] for one in sums], axis=0
                ).astype(BF16)
        return carry

    lax.fori_loop(0, rows // 16, step, 0, unroll=True)


def build_dense(place, blocks, weights, width):
    groups = len(blocks)
    part = blocks[0].shape
    rows = part[0] * groups
    vmem = pl.BlockSpec(memory_space=pltpu.VMEM)
    dense = ()
    for back, block in enumerate(blocks):
        early = {groups - 2: weights[:1], groups - 1: weights[1:]}.get(back, ())
        dense = pl.pallas_call(
            functools.partial(dense_kernel, back=back, groups=groups),
            out_shape=(jax.ShapeDtypeStruct((rows, width), BF16),) * 2,
            grid=(1,),
            in_specs=[
                pl.BlockSpec(memory_space=pltpu.SMEM),
                pl.BlockSpec(part, lambda i: (0, 0)),
            ]
            + [vmem] * len(dense)
            + [vmem] * len(early),
            out_specs=(vmem, vmem),
            input_output_aliases={2 + k: k for k in range(len(dense))},
            compiler_params=pltpu.CompilerParams(vmem_limit_bytes=DENSE_VMEM),
            cost_estimate=pl.CostEstimate(
                flops=1_000_000_000, bytes_accessed=3_000_000, transcendentals=0
            ),
            name="build_dense",
        )(place, block, *dense, *early)
    return dense


def sum_kernel(parts_ref, out_ref):
    count, _, columns = parts_ref.shape
    block = 4 * LANES
    for first in range(0, columns, block):
        at = slice(first, first + block)
        total = parts_ref[0, :, at].astype(F32)
        for part in range(1, count):
            total = total + parts_ref[part, :, at].astype(F32)
        out_ref[:, at] = total.astype(out_ref.dtype)


def sum_parts(parts):
    vmem = pl.BlockSpec(memory_space=pltpu.VMEM)
    return pl.pallas_call(
        sum_kernel,
        out_shape=jax.ShapeDtypeStruct(parts.shape[1:], BF16),
        in_specs=[vmem],
        out_specs=vmem,
        compiler_params=pltpu.CompilerParams(vmem_limit_bytes=4 << 20),
        name="sum_parts",
    )(parts)


def swap(values):
    return lax.ppermute(values, "core", [(0, 1), (1, 0)])


def from_others(values, axes):
    count = lax.axis_size(axes)
    return [
        lax.ppermute(values, axes, [(i, (i + step) % count) for i in range(count)])
        for step in range(1, count)
    ]


def near_exchange(values):
    return lax.all_to_all(values, NEAR, 0, 0, tiled=True)


def far_sum(sent):
    one, two, three = [block.astype(F32) for block in from_others(sent, FAR)]
    return (sent.astype(F32) + two) + (one + three)


def near_gather(values):
    count = lax.axis_size(NEAR)
    sent = jnp.broadcast_to(values[None], (count,) + values.shape)
    return near_exchange(sent).reshape(-1, values.shape[-1])


def on_device(peak_bins, peak_values, enc_weight, enc_bias, dec_weight):
    width, hidden_size = enc_weight.shape
    core = lax.axis_index("core")
    group = lax.axis_index(SPECTRA_AXES)
    position = lax.axis_index(NAMES)
    stride = lax.axis_size(SPECTRA_AXES)
    partner = position + (1 - 2 * core) * stride
    place = jnp.stack([position * width, partner * width, group]).astype(jnp.int32)
    packed = pack_peaks(core.reshape(1), peak_bins, peak_values)
    enc_weights = (enc_weight, swap(enc_weight))
    dec_weights = (dec_weight, swap(dec_weight))
    dense_own, dense_pair = build_dense(
        place, [packed] + from_others(packed, SPECTRA_AXES), enc_weights, width
    )
    dense = (dense_own, dense_pair)

    def encode(block, weight):
        return jnp.dot(block, weight, preferred_element_type=F32)

    def residual(block, hidden, weight):
        recon = jnp.dot(hidden, weight, preferred_element_type=F32)
        return (recon - block.astype(F32)).astype(BF16)

    def decode_back(resid, weight):
        return lax.dot_general(
            resid, weight, (((1,), (1,)), ((), ())), preferred_element_type=F32
        )

    def rows_dot(left, right):
        return lax.dot_general(
            left, right, (((0,), (0,)), ((), ())), preferred_element_type=F32
        )

    def near_parts(rows):
        return near_exchange(rows.astype(BF16).reshape(lax.axis_size(NEAR), -1, hidden_size))

    parts = near_parts(sum(map(encode, dense, enc_weights)))
    pre = far_sum(sum_parts(parts)) + enc_bias
    hidden = near_gather(activation(pre).astype(BF16))
    resid = [
        lax.optimization_barrier(residual(block, hidden, weight))
        for block, weight in zip(dense, dec_weights)
    ]
    parts = near_parts(sum(map(decode_back, resid, dec_weights)))
    grad_dec = rows_dot(
        jnp.concatenate([hidden, swap(hidden)]), jnp.concatenate([resid[0], swap(resid[1])])
    ).astype(BF16)
    parts, grad_dec, dense_sent = lax.optimization_barrier((parts, grad_dec, dense_pair))
    back, dense_other = lax.optimization_barrier((far_sum(sum_parts(parts)), swap(dense_sent)))
    dpre = near_gather(slope_times(pre, back))
    grad_own = lax.optimization_barrier(rows_dot(dense_own, dpre))
    grad_enc = (rows_dot(dense_other, swap(dpre)) + grad_own).astype(BF16)
    return (grad_enc, grad_dec)


def solution(mesh):
    fine = Mesh(mesh.devices.reshape(SHAPE), NAMES)
    placed = (
        P(SPECTRA_AXES, None),
        P(SPECTRA_AXES, None),
        P(NAMES, None),
        P(),
        P(None, NAMES),
    )
    return jax.shard_map(
        on_device,
        mesh=fine,
        in_specs=placed,
        out_specs=(P(NAMES, None), P(None, NAMES)),
        check_vma=False,
    )
```

```python
import functools

import jax
import jax.numpy as jnp
from jax import lax
from jax.experimental import pallas as pl
from jax.experimental.pallas import tpu as pltpu
from jax.sharding import Mesh
from jax.sharding import PartitionSpec as P

SHAPE = (4, 2, 4, 2, 2, 2)
NAMES = ("x", "zhi", "y", "core", "zp", "zq")
NEAR = ("x", "y", "zq")
FAR = ("zhi", "zp")
SPECTRA_AXES = ("zp", "zq")
LANES = 128
STEP = 512
PACK_VMEM = 60 << 20
DENSE_VMEM = 8 << 20
BF16 = jnp.bfloat16
F32 = jnp.float32


def activation(values):
    return jax.nn.gelu(values, approximate=True)


def slope_times(pre, back):
    _, pullback = jax.vjp(activation, pre)
    return pullback(back)[0].astype(BF16)


def pack_kernel(core_ref, bins_ref, values_ref, out_ref):
    rows, lanes = out_ref.shape
    peaks = lanes // 3
    first = pl.multiple_of(core_ref[0] * rows, rows)
    bins = bins_ref[pl.ds(first, rows), :]
    out_ref[:, :peaks] = ((bins >> 9) - 192).astype(F32).astype(BF16)
    out_ref[:, peaks : 2 * peaks] = ((bins & (STEP - 1)) - 256).astype(F32).astype(BF16)
    out_ref[:, 2 * peaks :] = values_ref[pl.ds(first, rows), :]


def pack_peaks(core, bins, values):
    rows, peaks = bins.shape
    whole = pl.BlockSpec(bins.shape, lambda i: (0, 0))
    packed = (rows // 2, 3 * peaks)
    return pl.pallas_call(
        pack_kernel,
        out_shape=jax.ShapeDtypeStruct(packed, BF16),
        grid=(1,),
        in_specs=[pl.BlockSpec(memory_space=pltpu.SMEM), whole, whole],
        out_specs=pl.BlockSpec(packed, lambda i: (0, 0)),
        compiler_params=pltpu.CompilerParams(vmem_limit_bytes=PACK_VMEM),
        name="pack_peaks",
    )(core, bins, values)


def dense_rows(bins, values, firsts, tiles, consts):
    lane, upper, which = consts
    low = (bins & (LANES - 1)).astype(BF16)
    twice = jnp.concatenate([values, values], axis=0).astype(BF16)
    picked = []
    for first in firsts:
        local = bins - first
        inside = (local >= 0) & (local < tiles * LANES)
        high = jnp.where(inside, local >> 7, -9).astype(F32)
        high = jnp.concatenate([high, high], axis=0).astype(BF16) - upper
        for tile in range(0, tiles, 2):
            picked.append(jnp.where(high == tile, twice, jnp.zeros_like(twice)))
    left = jnp.concatenate(
        [
            jnp.concatenate(
                [jnp.where(which == row, one, jnp.zeros_like(one)) for one in picked], axis=0
            )
            for row in range(8)
        ],
        axis=1,
    )
    ones = jnp.ones((LANES, LANES), BF16)
    right = jnp.concatenate(
        [jnp.where(low[row][None, :] == lane, ones, jnp.zeros_like(ones)) for row in range(8)],
        axis=1,
    )
    return lax.dot_general(left, right, (((1,), (1,)), ((), ())), preferred_element_type=F32)


def dense_kernel(place_ref, packed_ref, *refs, back, groups):
    own_ref, pair_ref = refs[-2:]
    rows, lanes = packed_ref.shape
    peaks = lanes // 3
    tiles = own_ref.shape[1] // LANES
    firsts = (place_ref[0], place_ref[1])
    lane = lax.broadcasted_iota(jnp.int32, (LANES, 1), 0).astype(BF16)
    row16 = lax.broadcasted_iota(jnp.int32, (16, LANES), 0)
    consts = (lane, (row16 >= 8).astype(jnp.int32).astype(BF16), (row16 & 7).astype(BF16))
    base = lax.rem(place_ref[2] + groups - back, groups) * rows

    def step(group, carry):
        row = pl.multiple_of(group * 16, 16)
        block = packed_ref[pl.ds(row, 16), :].astype(F32)
        bins = (block[:, :peaks].astype(jnp.int32) + 192) * STEP
        bins = bins + block[:, peaks : 2 * peaks].astype(jnp.int32) + 256
        values = block[:, 2 * peaks :]
        sums = [
            dense_rows(bins[h : h + 8], values[h : h + 8], firsts, tiles, consts)
            for h in (0, 8)
        ]
        target = pl.multiple_of(base + row, 16)
        for ref, skip in ((own_ref, 0), (pair_ref, tiles)):
            for tile in range(tiles):
                at = (skip + tile) * 8
                ref[pl.ds(target, 16), tile * LANES : (tile + 1) * LANES] = jnp.concatenate(
                    [one[at : at + 8] for one in sums], axis=0
                ).astype(BF16)
        return carry

    lax.fori_loop(0, rows // 16, step, 0, unroll=True)


def build_dense(place, blocks, weights, width):
    groups = len(blocks)
    part = blocks[0].shape
    rows = part[0] * groups
    vmem = pl.BlockSpec(memory_space=pltpu.VMEM)
    dense = ()
    for back, block in enumerate(blocks):
        early = {groups - 2: weights[:1], groups - 1: weights[1:]}.get(back, ())
        dense = pl.pallas_call(
            functools.partial(dense_kernel, back=back, groups=groups),
            out_shape=(jax.ShapeDtypeStruct((rows, width), BF16),) * 2,
            grid=(1,),
            in_specs=[
                pl.BlockSpec(memory_space=pltpu.SMEM),
                pl.BlockSpec(part, lambda i: (0, 0)),
            ]
            + [vmem] * len(dense)
            + [vmem] * len(early),
            out_specs=(vmem, vmem),
            input_output_aliases={2 + k: k for k in range(len(dense))},
            compiler_params=pltpu.CompilerParams(vmem_limit_bytes=DENSE_VMEM),
            cost_estimate=pl.CostEstimate(
                flops=1_000_000_000, bytes_accessed=3_000_000, transcendentals=0
            ),
            name="build_dense",
        )(place, block, *dense, *early)
    return dense


def sum_kernel(parts_ref, out_ref):
    count, _, columns = parts_ref.shape
    block = 4 * LANES
    for first in range(0, columns, block):
        at = slice(first, first + block)
        total = parts_ref[0, :, at].astype(F32)
        for part in range(1, count):
            total = total + parts_ref[part, :, at].astype(F32)
        out_ref[:, at] = total.astype(out_ref.dtype)


def sum_parts(parts):
    vmem = pl.BlockSpec(memory_space=pltpu.VMEM)
    return pl.pallas_call(
        sum_kernel,
        out_shape=jax.ShapeDtypeStruct(parts.shape[1:], BF16),
        in_specs=[vmem],
        out_specs=vmem,
        compiler_params=pltpu.CompilerParams(vmem_limit_bytes=4 << 20),
        name="sum_parts",
    )(parts)


def swap(values):
    return lax.ppermute(values, "core", [(0, 1), (1, 0)])


def from_others(values, axes):
    count = lax.axis_size(axes)
    return [
        lax.ppermute(values, axes, [(i, (i + step) % count) for i in range(count)])
        for step in range(1, count)
    ]


def near_exchange(values):
    return lax.all_to_all(values, NEAR, 0, 0, tiled=True)


def far_sum(sent):
    one, two, three = [block.astype(F32) for block in from_others(sent, FAR)]
    return (one + three) + (sent.astype(F32) + two)


def near_gather(values):
    count = lax.axis_size(NEAR)
    sent = jnp.broadcast_to(values[None], (count,) + values.shape)
    return near_exchange(sent).reshape(-1, values.shape[-1])


def on_device(peak_bins, peak_values, enc_weight, enc_bias, dec_weight):
    width, hidden_size = enc_weight.shape
    core = lax.axis_index("core")
    group = lax.axis_index(SPECTRA_AXES)
    position = lax.axis_index(NAMES)
    stride = lax.axis_size(SPECTRA_AXES)
    partner = position + (1 - 2 * core) * stride
    place = jnp.stack([position * width, partner * width, group]).astype(jnp.int32)
    packed = pack_peaks(core.reshape(1), peak_bins, peak_values)
    enc_weights = (enc_weight, swap(enc_weight))
    dec_weights = (dec_weight, swap(dec_weight))
    dense_own, dense_pair = build_dense(
        place, [packed] + from_others(packed, SPECTRA_AXES), enc_weights, width
    )
    dense = (dense_own, dense_pair)

    def encode(block, weight):
        return jnp.dot(block, weight, preferred_element_type=F32)

    def residual(block, hidden, weight):
        recon = jnp.dot(hidden, weight, preferred_element_type=F32)
        return (recon - block.astype(F32)).astype(BF16)

    def decode_back(resid, weight):
        return lax.dot_general(
            resid, weight, (((1,), (1,)), ((), ())), preferred_element_type=F32
        )

    def rows_dot(left, right):
        return lax.dot_general(
            left, right, (((0,), (0,)), ((), ())), preferred_element_type=F32
        )

    def near_parts(rows):
        return near_exchange(rows.astype(BF16).reshape(lax.axis_size(NEAR), -1, hidden_size))

    parts = near_parts(sum(map(encode, dense, enc_weights)))
    pre = far_sum(sum_parts(parts)) + enc_bias
    hidden = near_gather(activation(pre).astype(BF16))
    resid = [
        lax.optimization_barrier(residual(block, hidden, weight))
        for block, weight in zip(dense, dec_weights)
    ]
    parts = near_parts(sum(map(decode_back, resid, dec_weights)))
    grad_dec = rows_dot(
        jnp.concatenate([hidden, swap(hidden)]), jnp.concatenate([resid[0], swap(resid[1])])
    ).astype(BF16)
    parts, grad_dec, dense_sent = lax.optimization_barrier((parts, grad_dec, dense_pair))
    back, dense_other = lax.optimization_barrier((far_sum(sum_parts(parts)), swap(dense_sent)))
    dpre = near_gather(slope_times(pre, back))
    grad_own = lax.optimization_barrier(rows_dot(dense_own, dpre))
    grad_enc = (rows_dot(dense_other, swap(dpre)) + grad_own).astype(BF16)
    return (grad_enc, grad_dec)


def solution(mesh):
    fine = Mesh(mesh.devices.reshape(SHAPE), NAMES)
    placed = (
        P(SPECTRA_AXES, None),
        P(SPECTRA_AXES, None),
        P(NAMES, None),
        P(),
        P(None, NAMES),
    )
    return jax.shard_map(
        on_device,
        mesh=fine,
        in_specs=placed,
        out_specs=(P(NAMES, None), P(None, NAMES)),
        check_vma=False,
    )
```
